32 devices in a mesh: seq: 8 (over y, x, core), fsdp: 4 (over z).
Axes of the slice: x: 2, y: 2, z: 4, core: 2. Of those that a mesh axis runs over, the one named last changes fastest.
Arguments:
- tokens: bfloat16 [16, 1024, 1024], P('fsdp', 'seq'), may hold values from -6 to 6
- pre_gain: bfloat16 [2, 1024], P(None, 'fsdp'), may hold values from 0.5 to 1.5
- in_weight: bfloat16 [2, 1024, 4384], P(None, 'fsdp'), may hold values from -0.1875 to 0.1875
- filter_weight: bfloat16 [2, 4, 2304], P(None, None, 'fsdp'), may hold values from -3 to 3
- filter_bias: bfloat16 [2, 2304], P(None, 'fsdp'), may hold values from -3 to 3
- step_bias: float32 [2, 32], replicated, may hold values from -6 to -2
- decay_log: float32 [2, 32], replicated, may hold values from 0 to 2.77
- skip_scale: float32 [2, 32], replicated, may hold values from 0.5 to 1.5
- inner_gain: bfloat16 [2, 2048], P(None, 'fsdp'), may hold values from 0.5 to 1.5
- out_weight: bfloat16 [2, 2048, 1024], P(None, 'fsdp'), may hold values from -0.125 to 0.125
- cotangent: bfloat16 [16, 1024, 1024], P('fsdp', 'seq'), may hold values from -6 to 6
Outputs:
- output: bfloat16 [16, 1024, 1024], P('fsdp', 'seq')
- token_grad: bfloat16 [16, 1024, 1024], P('fsdp', 'seq')
- pre_gain_grad: float32 [2, 1024], P(None, 'fsdp')
- in_weight_grad: float32 [2, 1024, 4384], P(None, 'fsdp')
- filter_weight_grad: float32 [2, 4, 2304], P(None, None, 'fsdp')
- filter_bias_grad: float32 [2, 2304], P(None, 'fsdp')
- step_bias_grad: float32 [2, 32], replicated
- decay_log_grad: float32 [2, 32], replicated
- skip_scale_grad: float32 [2, 32], replicated
- inner_gain_grad: float32 [2, 2048], P(None, 'fsdp')
- out_weight_grad: float32 [2, 2048, 1024], P(None, 'fsdp')
The draws below stay inside these ranges and needn't reach their ends.
All inputs are finite; a program needn't handle non-finite values.
Results may differ from the reference program's by a relative error of at most 0.02.
Values may be sent and summed in bfloat16 or wider, within the bound.
A program may use at most 256 MiB of HBM per device.

```python
from functools import partial
import jax
import jax.numpy as jnp
from jax import lax

D = 1024
DI = 2048
NH = 32
HEAD = 64
NS = 128
CONV_K = 4
BLOCK = 256
XBC = 2304
PROJ = 4384
LAYERS = 2
SEQ_LEN = 1024
SEQS = 16


def block_scale(rng, dims, pieces, smallest, high):
    def one(dim, shards_of):
        steps = jax.random.uniform(jax.random.fold_in(jax.random.fold_in(rng, 6), dim), (shards_of,), jnp.float32, smallest / len(pieces), high / len(pieces))
        return jnp.repeat(jnp.exp(steps), dims[dim] // shards_of).reshape((-1,) + (1,) * (len(dims) - dim - 1))

    level = one(*pieces[0])
    for cut in pieces[1:]:
        level = level * one(*cut)
    return level


def bell_draw(rng, shape, scale, most, shards=(), held_as=jnp.bfloat16):
    factor_of = block_scale(rng, shape, shards, -0.22, 0.18) if shards else 1.0
    drawn = jax.random.normal(rng, shape, jnp.float32) * scale * factor_of
    return jnp.minimum(jnp.maximum(drawn, -most), most).astype(held_as)


def setup_inputs(seed: int = 0) -> dict:
    arg_keys = jax.random.split(jax.random.key(seed), 12)
    tokens = bell_draw(arg_keys[0], (SEQS, SEQ_LEN, D), 1.0, 6.0, ((0, 4), (1, 8)))
    pre_gain = jnp.clip(1.0 + 0.1 * jax.random.normal(arg_keys[1], (LAYERS, D), jnp.float32), 0.5, 1.5).astype(jnp.bfloat16)
    in_weight = bell_draw(arg_keys[2], (LAYERS, D, PROJ), D ** -0.5, 0.1875, ((1, 4),))
    filter_weight = bell_draw(arg_keys[3], (LAYERS, CONV_K, XBC), CONV_K ** -0.5, 3.0, ((2, 4),))
    filter_bias = bell_draw(arg_keys[4], (LAYERS, XBC), 0.5, 3.0, ((1, 4),))
    step_bias = jnp.clip(jax.random.uniform(arg_keys[5], (LAYERS, NH), jnp.float32, -6.0, -2.0), -6.0, -2.0)
    decay_log = jnp.clip(jax.random.uniform(arg_keys[6], (LAYERS, NH), jnp.float32, 0.0, 2.77), 0.0, 2.77)
    skip_scale = jnp.clip(jax.random.uniform(arg_keys[7], (LAYERS, NH), jnp.float32, 0.5, 1.5), 0.5, 1.5)
    inner_gain = jnp.clip(1.0 + 0.1 * jax.random.normal(arg_keys[8], (LAYERS, DI), jnp.float32), 0.5, 1.5).astype(jnp.bfloat16)
    out_weight = bell_draw(arg_keys[9], (LAYERS, DI, D), DI ** -0.5, 0.125, ((1, 4),))
    cotangent = bell_draw(arg_keys[10], (SEQS, SEQ_LEN, D), 1.0, 6.0, ((0, 4), (1, 8)))
    return {"tokens": tokens, "pre_gain": pre_gain, "in_weight": in_weight, "filter_weight": filter_weight, "filter_bias": filter_bias, "step_bias": step_bias, "decay_log": decay_log, "skip_scale": skip_scale, "inner_gain": inner_gain, "out_weight": out_weight, "cotangent": cotangent}


EPSILON = 1e-05
HIGHEST = lax.Precision.HIGHEST

@jax.custom_vjp
def low(v):
    return lax.optimization_barrier(v.astype(jnp.bfloat16)).astype(jnp.float32)

@jax.custom_vjp
def low_back(v):
    return v

def low_keep(v):
    return (low(v), None)

def low_pass(kept, grad):
    return (grad,)

def back_keep(v):
    return (v, None)

def back_low(kept, grad):
    return (low(grad),)
low.defvjp(low_keep, low_pass)
low_back.defvjp(back_keep, back_low)

def root_scale(values, gain):
    return values * lax.rsqrt(lax.optimization_barrier(jnp.mean(values * values, axis=-1, keepdims=True)) + EPSILON) * gain

def causal_filter(raw_rows, kernel, offset):
    tap_count = kernel.shape[0]
    length = raw_rows.shape[0]
    padded = jnp.pad(raw_rows, ((tap_count - 1, 0), (0, 0)))
    summed = offset
    for tap_number in range(tap_count):
        summed = summed + padded[tap_number:tap_number + length] * kernel[tap_number]
    return jax.nn.silu(summed)

def head_scan(inner_seq, step_seq, cumul_seq, skip_value, entry_rows, exit_rows):
    inner_prod = low_back(jnp.einsum('cin,cjn->cij', exit_rows, entry_rows, precision=HIGHEST))
    row_index = lax.broadcasted_iota(jnp.int32, (BLOCK, BLOCK), 0)
    column_index = lax.broadcasted_iota(jnp.int32, (BLOCK, BLOCK), 1)
    causal = row_index >= column_index
    spread = cumul_seq[:, :, None] - cumul_seq[:, None, :]
    scores = low(jnp.where(causal, inner_prod * jnp.exp(jnp.where(causal, spread, 0.0)) * step_seq[:, None, :], 0.0))
    within = jnp.einsum('cij,cjp->cip', scores, inner_seq, precision=HIGHEST)
    writes = low((jnp.exp(cumul_seq[:, -1:] - cumul_seq) * step_seq)[:, :, None] * entry_rows)
    states = low_back(jnp.einsum('cjn,cjp->cnp', writes, inner_seq, precision=HIGHEST))
    totals = cumul_seq[:, -1]
    running = jnp.cumsum(totals)
    before = running - totals
    blocks = totals.shape[0]
    later_mask = lax.broadcasted_iota(jnp.int32, (blocks, blocks), 0) > lax.broadcasted_iota(jnp.int32, (blocks, blocks), 1)
    block_gaps = before[:, None] - running[None, :]
    decay_matrix = jnp.where(later_mask, jnp.exp(jnp.where(later_mask, block_gaps, 0.0)), 0.0)
    carried = low(jnp.einsum('cd,dnp->cnp', decay_matrix, states, precision=HIGHEST))
    read_rows = low(jnp.exp(cumul_seq)[:, :, None] * exit_rows)
    across = jnp.einsum('cin,cnp->cip', read_rows, carried, precision=HIGHEST)
    return within + across + skip_value * inner_seq

def mamba_layer(residual, layer_params):
    gain_in, weight_in, kernel, offset, bias_value, decay_rate, skip_value, gain_mid, weight_out = layer_params
    length = residual.shape[0]
    blocks = length // BLOCK
    normed = low(root_scale(residual, gain_in))
    projected = low_back(low(jnp.dot(normed, weight_in, precision=HIGHEST)))
    gate_raw = projected[:, :DI]
    filtered = low(causal_filter(projected[:, DI:DI + XBC], kernel, offset))
    inner_rows = filtered[:, :DI]
    entry_rows = filtered[:, DI:DI + NS].reshape(blocks, BLOCK, NS)
    exit_rows = filtered[:, DI + NS:DI + XBC].reshape(blocks, BLOCK, NS)
    step_size = jax.nn.softplus(projected[:, DI + XBC:] + bias_value)
    log_rate = -jnp.exp(decay_rate) * step_size
    cumulative = jnp.cumsum(log_rate.reshape(blocks, BLOCK, NH), axis=1)
    inner_heads = jnp.transpose(inner_rows.reshape(blocks, BLOCK, NH, HEAD), (2, 0, 1, 3))
    step_heads = jnp.transpose(step_size.reshape(blocks, BLOCK, NH), (2, 0, 1))
    cumul_heads = jnp.transpose(cumulative, (2, 0, 1))
    scan_head = jax.checkpoint(partial(head_scan, entry_rows=entry_rows, exit_rows=exit_rows))
    mixed_heads = lax.map(lambda members: scan_head(members[0], members[1], members[2], members[3]), (inner_heads, step_heads, cumul_heads, skip_value))
    mixed_rows = jnp.transpose(mixed_heads, (1, 2, 0, 3)).reshape(length, DI)
    mixed_rows = low_back(low(mixed_rows))
    gated_rows = low(root_scale(mixed_rows * jax.nn.silu(gate_raw), gain_mid))
    branch = low_back(jnp.dot(gated_rows, weight_out, precision=HIGHEST))
    return residual + branch

def reference(tokens, pre_gain, in_weight, filter_weight, filter_bias, step_bias, decay_log, skip_scale, inner_gain, out_weight, cotangent):
    weights = tuple((weight_item.astype(jnp.float32) for weight_item in (pre_gain, in_weight, filter_weight, filter_bias, step_bias, decay_log, skip_scale, inner_gain, out_weight)))

    def forward(inputs, params):

        def one_sequence(sequence):
            residual = sequence
            for layer_number in range(LAYERS):
                residual = mamba_layer(residual, tuple((item[layer_number] for item in params)))
            return residual
        return lax.map(jax.checkpoint(one_sequence), inputs)
    result, pullback = jax.vjp(forward, tokens.astype(jnp.float32), weights)
    token_grad, gradients = pullback(cotangent.astype(jnp.float32))
    return (result.astype(jnp.bfloat16), token_grad.astype(jnp.bfloat16), gradients[0], gradients[1], gradients[2], gradients[3], gradients[4], gradients[5], gradients[6], gradients[7], gradients[8])
```

```python
import jax
import jax.numpy as jnp
from jax import lax
from jax.sharding import Mesh
from jax.sharding import PartitionSpec as P

DI = 2048
NH = 32
HEAD = 64
NS = 128
CONV_K = 4
BLOCK = 256


EPSILON = 1e-05
HIGHEST = lax.Precision.HIGHEST
HALF_TYPE = jnp.bfloat16
FULL_TYPE = jnp.float32


def root_scale(values, gain):
    return values * lax.rsqrt(jnp.mean(values * values, axis=-1, keepdims=True) + EPSILON) * gain


def gated_norm(mixed_rows, gate_rows, gain):
    return root_scale(mixed_rows * jax.nn.silu(gate_rows), gain)


def causal_filter(raw_rows, kernel, offset):
    tap_count = kernel.shape[0]
    length = raw_rows.shape[0]
    padded = jnp.pad(raw_rows, ((tap_count - 1, 0), (0, 0)))
    summed = offset
    for tap_number in range(tap_count):
        summed = summed + padded[tap_number : tap_number + length] * kernel[tap_number]
    return jax.nn.silu(summed)


def head_inputs(
    inner_raw,
    step_raw,
    shared_raw,
    kernel_inner,
    offset_inner,
    kernel_shared,
    offset_shared,
    bias_local,
    decay_local,
):
    inner_filtered = causal_filter(inner_raw, kernel_inner, offset_inner)
    shared_filtered = causal_filter(shared_raw, kernel_shared, offset_shared)
    step_size = jax.nn.softplus(step_raw + bias_local)
    log_rate = -jnp.exp(decay_local) * step_size
    blocks = log_rate.shape[0] // BLOCK
    step_blocks = step_size.reshape(blocks, BLOCK, step_size.shape[1])
    rate_blocks = log_rate.reshape(blocks, BLOCK, log_rate.shape[1])
    lower = jnp.tri(BLOCK, dtype=FULL_TYPE)
    cumulative = jnp.einsum("ij,cjh->cih", lower, rate_blocks, precision=HIGHEST)
    return (inner_filtered, shared_filtered, step_blocks, cumulative)


def mixing(inner_prod, entry_full, exit_full, cumulative, step_blocks):
    cumul_heads = jnp.transpose(cumulative, (0, 2, 1))
    step_heads = jnp.transpose(step_blocks, (0, 2, 1))
    row_index = lax.broadcasted_iota(jnp.int32, (BLOCK, BLOCK), 0)
    column_index = lax.broadcasted_iota(jnp.int32, (BLOCK, BLOCK), 1)
    causal = row_index >= column_index
    spread = cumul_heads[..., :, None] - cumul_heads[..., None, :]
    scores = jnp.where(
        causal, inner_prod[:, None] * jnp.exp(jnp.where(causal, spread, 0.0)) * step_heads[..., None, :], 0.0
    )
    writes = (jnp.exp(cumul_heads[..., -1:] - cumul_heads) * step_heads)[..., None] * entry_full[
        :, None
    ]
    read_rows = jnp.exp(cumul_heads)[..., None] * exit_full[:, None]
    return (scores, writes, read_rows)


def carry_states(cumulative, states):
    totals = jnp.exp(cumulative[:, -1, :])
    carried = jnp.zeros_like(states[0])
    entering = []
    for block_number in range(states.shape[0]):
        entering.append(carried)
        carried = totals[block_number][:, None, None] * carried + states[block_number]
    return jnp.stack(entering)


def split_halves(inner_filtered, shared_filtered, blocks, head_count):
    inner_half = inner_filtered.astype(HALF_TYPE).reshape(blocks, BLOCK, head_count, HEAD)
    shared_half = shared_filtered.astype(HALF_TYPE).reshape(blocks, BLOCK, 2 * NS)
    return (inner_half, shared_half[..., :NS], shared_half[..., NS:])


def head_forward(inner_raw, step_raw, shared_raw, params):
    (
        kernel_inner,
        offset_inner,
        kernel_shared,
        offset_shared,
        bias_local,
        decay_local,
        skip_local,
    ) = params
    inner_filtered, shared_filtered, step_blocks, cumulative = head_inputs(
        inner_raw.astype(FULL_TYPE),
        step_raw.astype(FULL_TYPE),
        shared_raw.astype(FULL_TYPE),
        kernel_inner,
        offset_inner,
        kernel_shared,
        offset_shared,
        bias_local,
        decay_local,
    )
    blocks, head_count = (step_blocks.shape[0], step_blocks.shape[2])
    inner_half, entry_half, exit_half = split_halves(
        inner_filtered, shared_filtered, blocks, head_count
    )
    inner_prod = jnp.einsum("cin,cjn->cij", exit_half, entry_half, preferred_element_type=FULL_TYPE)
    scores, writes, read_rows = mixing(
        inner_prod, entry_half.astype(FULL_TYPE), exit_half.astype(FULL_TYPE), cumulative, step_blocks
    )
    within = jnp.einsum(
        "chij,cjhp->cihp", scores.astype(HALF_TYPE), inner_half, preferred_element_type=FULL_TYPE
    )
    states = jnp.einsum(
        "chjn,cjhp->chnp", writes.astype(HALF_TYPE), inner_half, preferred_element_type=FULL_TYPE
    )
    carried = carry_states(cumulative, states).astype(HALF_TYPE)
    across = jnp.einsum(
        "chin,chnp->cihp", read_rows.astype(HALF_TYPE), carried, preferred_element_type=FULL_TYPE
    )
    mixed_rows = within + across + skip_local[:, None] * inner_half.astype(FULL_TYPE)
    return mixed_rows.reshape(blocks * BLOCK, head_count * HEAD).astype(HALF_TYPE)


def head_backward(inner_raw, step_raw, shared_raw, mixed_grad, params):
    (
        kernel_inner,
        offset_inner,
        kernel_shared,
        offset_shared,
        bias_local,
        decay_local,
        skip_local,
    ) = params
    prepared, prep_back = jax.vjp(
        head_inputs,
        inner_raw.astype(FULL_TYPE),
        step_raw.astype(FULL_TYPE),
        shared_raw.astype(FULL_TYPE),
        kernel_inner,
        offset_inner,
        kernel_shared,
        offset_shared,
        bias_local,
        decay_local,
    )
    inner_filtered, shared_filtered, step_blocks, cumulative = prepared
    blocks, head_count = (step_blocks.shape[0], step_blocks.shape[2])
    inner_half, entry_half, exit_half = split_halves(
        inner_filtered, shared_filtered, blocks, head_count
    )
    inner_prod = jnp.einsum("cin,cjn->cij", exit_half, entry_half, preferred_element_type=FULL_TYPE)
    mixes, mix_back = jax.vjp(
        mixing,
        inner_prod,
        entry_half.astype(FULL_TYPE),
        exit_half.astype(FULL_TYPE),
        cumulative,
        step_blocks,
    )
    scores_half = mixes[0].astype(HALF_TYPE)
    writes_half = mixes[1].astype(HALF_TYPE)
    reads_half = mixes[2].astype(HALF_TYPE)
    states = jnp.einsum(
        "chjn,cjhp->chnp", writes_half, inner_half, preferred_element_type=FULL_TYPE
    )
    carried, carry_back = jax.vjp(carry_states, cumulative, states)
    carried_half = carried.astype(HALF_TYPE)
    grad_half = mixed_grad.reshape(blocks, BLOCK, head_count, HEAD)
    grad_full = grad_half.astype(FULL_TYPE)
    skip_grad = jnp.sum(grad_full * inner_half.astype(FULL_TYPE), axis=(0, 1, 3))
    reads_grad = jnp.einsum(
        "cihp,chnp->chin", grad_half, carried_half, preferred_element_type=FULL_TYPE
    )
    carried_grad = jnp.einsum(
        "chin,cihp->chnp", reads_half, grad_half, preferred_element_type=FULL_TYPE
    )
    cumul_grad, states_grad = carry_back(carried_grad)
    states_half = states_grad.astype(HALF_TYPE)
    writes_grad = jnp.einsum(
        "chnp,cjhp->chjn", states_half, inner_half, preferred_element_type=FULL_TYPE
    )
    scores_grad = jnp.einsum(
        "cihp,cjhp->chij", grad_half, inner_half, preferred_element_type=FULL_TYPE
    )
    inner_grad = skip_local[:, None] * grad_full
    inner_grad = inner_grad + jnp.einsum(
        "chjn,chnp->cjhp", writes_half, states_half, preferred_element_type=FULL_TYPE
    )
    inner_grad = inner_grad + jnp.einsum(
        "chij,cihp->cjhp", scores_half, grad_half, preferred_element_type=FULL_TYPE
    )
    prod_grad, entry_grad, exit_grad, cumul_more, step_grad = mix_back(
        (scores_grad, writes_grad, reads_grad)
    )
    prod_half = prod_grad.astype(HALF_TYPE)
    exit_grad = exit_grad + jnp.einsum(
        "cij,cjn->cin", prod_half, entry_half, preferred_element_type=FULL_TYPE
    )
    entry_grad = entry_grad + jnp.einsum(
        "cij,cin->cjn", prod_half, exit_half, preferred_element_type=FULL_TYPE
    )
    length = blocks * BLOCK
    shared_grad = jnp.concatenate([entry_grad, exit_grad], axis=-1).reshape(length, 2 * NS)
    raw_grads = prep_back(
        (
            inner_grad.reshape(length, head_count * HEAD),
            shared_grad,
            step_grad,
            cumul_grad + cumul_more,
        )
    )
    return raw_grads + (skip_grad,)


def gather_rows(shard):
    parts = lax.axis_size("chip") * lax.axis_size("core")
    part_rows = shard.shape[0] // parts
    part_number = lax.axis_index("chip") * lax.axis_size("core") + lax.axis_index("core")
    part = lax.dynamic_slice_in_dim(shard, part_number * part_rows, part_rows, 0)
    return lax.all_gather(part, ("fsdp", "chip", "core"), axis=0, tiled=True)


def scatter_rows(total):
    fsdp_count = lax.axis_size("fsdp")
    chips, cores = (lax.axis_size("chip"), lax.axis_size("core"))
    rows, columns = total.shape
    part_rows = rows // (fsdp_count * chips * cores)
    half = total.astype(HALF_TYPE)
    part = lax.psum_scatter(half, ("fsdp", "chip", "core"), scatter_dimension=0, tiled=True)
    return lax.all_gather(part, ("chip", "core"), axis=0, tiled=True)


def per_device(
    tokens,
    pre_gain,
    in_weight,
    filter_weight,
    filter_bias,
    step_bias,
    decay_log,
    skip_scale,
    inner_gain,
    out_weight,
    cotangent,
):
    core_count = lax.axis_size("core")
    position = lax.axis_index("core")
    fsdp_count = lax.axis_size("fsdp")
    heads_local = NH // core_count
    width_local = heads_local * HEAD
    layer_count = in_weight.shape[0]
    small_parts = (pre_gain, filter_weight, filter_bias, inner_gain)
    small_flat = jnp.concatenate([part.reshape(-1) for part in small_parts])
    small_all = lax.all_gather(small_flat, "fsdp", axis=0)
    small_full = []
    start = 0
    for part in small_parts:
        piece = small_all[:, start : start + part.size].reshape((fsdp_count,) + part.shape)
        start += part.size
        piece = jnp.moveaxis(piece, 0, -2)
        small_full.append(piece.reshape(part.shape[:-1] + (-1,)))
    weights_in = []
    weights_out = []
    for layer_number in range(layer_count):
        weights_in.append(gather_rows(in_weight[layer_number]))
        weights_out.append(gather_rows(out_weight[layer_number]))
    residual = lax.all_to_all(tokens, "chip", split_axis=0, concat_axis=0, tiled=True)
    cotangent = lax.all_to_all(cotangent, "chip", split_axis=0, concat_axis=0, tiled=True)
    residual = residual.astype(FULL_TYPE)
    chunks, chunk_rows = residual.shape[:2]
    length = chunks * core_count * chunk_rows
    saved = []
    for layer_number in range(layer_count):
        gain_in, kernel, offset, gain_mid = [part[layer_number] for part in small_full]
        weight_in = weights_in[layer_number]
        weight_out = weights_out[layer_number]
        normed = root_scale(residual, gain_in.astype(FULL_TYPE)).astype(HALF_TYPE)
        projected = jnp.einsum(
            "gsd,df->gsf", normed, weight_in, preferred_element_type=FULL_TYPE
        ).astype(HALF_TYPE)
        inner_raw = projected[..., DI : 2 * DI]
        inner_heads = lax.all_to_all(inner_raw, "core", split_axis=2, concat_axis=1, tiled=True)
        inner_heads = inner_heads.reshape(length, width_local)
        extra_all = lax.all_gather(projected[..., 2 * DI :], "core", axis=1, tiled=True)
        extra_all = extra_all.reshape(length, 2 * NS + NH)
        shared_all = extra_all[:, : 2 * NS]
        step_heads = lax.dynamic_slice_in_dim(
            extra_all, 2 * NS + position * heads_local, heads_local, 1
        )
        kernel_full = kernel.astype(FULL_TYPE)
        offset_full = offset.astype(FULL_TYPE)
        params = (
            lax.dynamic_slice_in_dim(kernel_full, position * width_local, width_local, 1),
            lax.dynamic_slice_in_dim(offset_full, position * width_local, width_local, 0),
            kernel_full[:, DI:],
            offset_full[DI:],
            lax.dynamic_slice_in_dim(
                step_bias[layer_number], position * heads_local, heads_local, 0
            ),
            lax.dynamic_slice_in_dim(
                decay_log[layer_number], position * heads_local, heads_local, 0
            ),
            lax.dynamic_slice_in_dim(
                skip_scale[layer_number], position * heads_local, heads_local, 0
            ),
        )
        mixed_heads = head_forward(inner_heads, step_heads, shared_all, params)
        mixed_heads = mixed_heads.reshape(chunks, core_count * chunk_rows, width_local)
        mixed_back = lax.all_to_all(mixed_heads, "core", split_axis=1, concat_axis=2, tiled=True)
        gated_rows = gated_norm(
            mixed_back.astype(FULL_TYPE),
            projected[..., :DI].astype(FULL_TYPE),
            gain_mid.astype(FULL_TYPE),
        ).astype(HALF_TYPE)
        residual_next = residual + jnp.einsum(
            "gsk,kd->gsd", gated_rows, weight_out, preferred_element_type=FULL_TYPE
        )
        saved.append(
            (
                residual,
                normed,
                projected,
                inner_heads,
                step_heads,
                shared_all,
                mixed_back,
                gated_rows,
                (gain_in, weight_in, gain_mid, weight_out),
                params,
            )
        )
        residual = residual_next
    output = residual.astype(HALF_TYPE)
    grad_residual = cotangent.astype(FULL_TYPE)
    small_terms = []
    in_terms = []
    out_terms = []
    for layer_number in reversed(range(layer_count)):
        (
            residual,
            normed,
            projected,
            inner_heads,
            step_heads,
            shared_all,
            mixed_back,
            gated_rows,
            weights,
            params,
        ) = saved[layer_number]
        gain_in, weight_in, gain_mid, weight_out = weights
        branch_grad = grad_residual.astype(HALF_TYPE)
        gated_grad = jnp.einsum(
            "gsd,kd->gsk", branch_grad, weight_out, preferred_element_type=FULL_TYPE
        )
        norm_value, norm_back = jax.vjp(
            gated_norm,
            mixed_back.astype(FULL_TYPE),
            projected[..., :DI].astype(FULL_TYPE),
            gain_mid.astype(FULL_TYPE),
        )
        mixed_grad, gate_grad, gain_mid_grad = norm_back(gated_grad)
        mixed_grad_heads = lax.all_to_all(
            mixed_grad.astype(HALF_TYPE), "core", split_axis=2, concat_axis=1, tiled=True
        ).reshape(length, width_local)
        weight_out_grad = jnp.einsum(
            "gsk,gsd->kd", gated_rows, branch_grad, preferred_element_type=FULL_TYPE
        )
        out_terms.append(scatter_rows(weight_out_grad))
        (
            inner_grad,
            step_grad,
            shared_grad,
            kernel_inner_grad,
            offset_inner_grad,
            kernel_shared_grad,
            offset_shared_grad,
            bias_grad,
            decay_grad,
            skip_grad,
        ) = head_backward(inner_heads, step_heads, shared_all, mixed_grad_heads, params)
        inner_back = lax.all_to_all(
            inner_grad.astype(HALF_TYPE).reshape(chunks, core_count * chunk_rows, width_local),
            "core",
            split_axis=1,
            concat_axis=2,
            tiled=True,
        )
        step_wide = lax.dynamic_update_slice_in_dim(
            jnp.zeros((length, NH), HALF_TYPE),
            step_grad.astype(HALF_TYPE),
            position * heads_local,
            1,
        )
        extra_grad = jnp.concatenate([shared_grad.astype(HALF_TYPE), step_wide], axis=1)
        extra_back = lax.psum_scatter(
            extra_grad.reshape(chunks, core_count * chunk_rows, 2 * NS + NH),
            "core",
            scatter_dimension=1,
            tiled=True,
        )
        projected_grad = jnp.concatenate(
            [gate_grad.astype(HALF_TYPE), inner_back, extra_back], axis=-1
        )
        weight_in_grad = jnp.einsum(
            "gsd,gsf->df", normed, projected_grad, preferred_element_type=FULL_TYPE
        )
        in_terms.append(scatter_rows(weight_in_grad))
        normed_grad = jnp.einsum(
            "gsf,df->gsd", projected_grad, weight_in, preferred_element_type=FULL_TYPE
        )
        pre_value, pre_back = jax.vjp(root_scale, residual, gain_in.astype(FULL_TYPE))
        residual_part, gain_in_grad = pre_back(normed_grad)
        grad_residual = grad_residual + residual_part
        kernel_grad = jnp.concatenate(
            [
                lax.dynamic_update_slice_in_dim(
                    jnp.zeros((CONV_K, DI), FULL_TYPE),
                    kernel_inner_grad,
                    position * width_local,
                    1,
                ),
                kernel_shared_grad,
            ],
            axis=1,
        )
        offset_grad = jnp.concatenate(
            [
                lax.dynamic_update_slice_in_dim(
                    jnp.zeros((DI,), FULL_TYPE),
                    offset_inner_grad,
                    position * width_local,
                    0,
                ),
                offset_shared_grad,
            ],
            axis=0,
        )
        heads_zero = jnp.zeros((NH,), FULL_TYPE)
        head_grads = [
            lax.dynamic_update_slice_in_dim(heads_zero, term_item, position * heads_local, 0)
            for term_item in (bias_grad, decay_grad, skip_grad)
        ]
        small_terms.append([gain_in_grad, kernel_grad, offset_grad, gain_mid_grad] + head_grads)
    layer_order = list(reversed(range(layer_count)))
    small_shapes = [item.shape for item in small_terms[0]]
    small_vector = jnp.concatenate(
        [item.reshape(-1) for number in layer_order for item in small_terms[number]]
    )
    small_rows = lax.psum(small_vector, ("chip", "core", "fsdp")).reshape(layer_count, -1)
    small_totals = []
    start = 0
    for shape in small_shapes:
        size = 1
        for extent in shape:
            size *= extent
        small_totals.append(small_rows[:, start : start + size].reshape((layer_count,) + shape))
        start += size
    shard_number = lax.axis_index("fsdp")
    for member_number in range(4):
        member = small_totals[member_number]
        width = member.shape[-1] // fsdp_count
        small_totals[member_number] = lax.dynamic_slice_in_dim(
            member, shard_number * width, width, member.ndim - 1
        )
    gain_in_total, kernel_total, offset_total, gain_mid_total = small_totals[:4]
    bias_total, decay_total, skip_total = small_totals[4:]
    output = lax.all_to_all(output, "chip", split_axis=0, concat_axis=0, tiled=True)
    token_grad = lax.all_to_all(
        grad_residual.astype(HALF_TYPE), "chip", split_axis=0, concat_axis=0, tiled=True
    )
    return (
        output,
        token_grad,
        gain_in_total,
        jnp.stack([in_terms[number] for number in layer_order]).astype(FULL_TYPE),
        kernel_total,
        offset_total,
        bias_total,
        decay_total,
        skip_total,
        gain_mid_total,
        jnp.stack([out_terms[number] for number in layer_order]).astype(FULL_TYPE),
    )


def solution(mesh):
    seq_count = mesh.shape["seq"]
    fsdp_count = mesh.shape["fsdp"]
    seq_spec = ("chip", "core")

    def whole(*arrays):
        chips = arrays[0].shape[0] // fsdp_count
        grid = mesh.devices.reshape(chips, seq_count // chips, fsdp_count)
        fine_mesh = Mesh(grid, ("chip", "core", "fsdp"))
        in_specs = (
            P("fsdp", seq_spec, None),
            P(None, "fsdp"),
            P(None, "fsdp", None),
            P(None, None, "fsdp"),
            P(None, "fsdp"),
            P(),
            P(),
            P(),
            P(None, "fsdp"),
            P(None, "fsdp", None),
            P("fsdp", seq_spec, None),
        )
        out_specs = (
            P("fsdp", seq_spec, None),
            P("fsdp", seq_spec, None),
            P(None, "fsdp"),
            P(None, "fsdp", None),
            P(None, None, "fsdp"),
            P(None, "fsdp"),
            P(),
            P(),
            P(),
            P(None, "fsdp"),
            P(None, "fsdp", None),
        )
        return jax.shard_map(
            per_device, mesh=fine_mesh, in_specs=in_specs, out_specs=out_specs, check_vma=False
        )(*arrays)

    return whole
```
